512 devices in a mesh: grp: 16 (over z), dev: 32 (over x, y, core).
Axes of the slice: x: 4, y: 4, z: 16, core: 2. Of those that a mesh axis runs over, the one named last changes fastest.
Arguments:
- stiff_rows: bfloat16 [512, 6, 384, 384], P(('grp', 'dev')), may hold values from -0.75 to 0.75
- stiff_iface: bfloat16 [512, 2, 384, 384], P(('grp', 'dev')), may hold values from -0.75 to 0.75
- columns: int32 [512, 6], P(('grp', 'dev')), may hold values from 0 to 31, as said below
- live_count: int32 [512], P(('grp', 'dev')), may hold values from 2 to 6
- aggregate: int32 [512], P(('grp', 'dev')), may hold values from 0 to 1
- prolong: bfloat16 [512, 384, 384], P(('grp', 'dev')), may hold values from -0.3125 to 0.3125
Outputs:
- coarse_band: float32 [12288, 2304], P(('grp', 'dev'))
The draws below stay inside these ranges and needn't reach their ends.
Inputs may be any that keep to these rules, and one draw needn't show every extreme that they name: The 6 columns of a row are distinct, the first is the row's own position p, and each lies within 3 positions of p around the cycle of 32 positions of the slab.
All inputs are finite; a program needn't handle non-finite values.
Results may differ from the reference program's by a relative error of at most 0.018.
Values may be sent and summed in bfloat16 or wider, within the bound.
A program may use at most 64 MiB of HBM per device.

```python
import jax
import jax.numpy as jnp
from jax import lax

NB = 384
SLOTS = 6
REACH = 3
COARSE = 2
FINE = 512
CROWS = 12288
N_GRP = 16
N_DEV = 32


def draw_columns(key, part):
    offsets = jnp.concatenate([jnp.arange(-REACH, 0, dtype=jnp.int32), jnp.arange(1, REACH + 1, dtype=jnp.int32)])
    row_keys = jax.random.split(key, FINE)
    orders = jax.vmap(lambda k: jax.random.permutation(k, 2 * REACH))(row_keys)
    chosen = offsets[orders[:, :SLOTS - 1]]
    shifts = jnp.concatenate([jnp.zeros((FINE, 1), jnp.int32), chosen], axis=1)
    position = (jnp.arange(FINE, dtype=jnp.int32) % N_DEV)[:, None]
    return ((position + shifts + N_DEV) % N_DEV).astype(jnp.int32)


def touch_ends(entries, rng, least, top_value):
    extent = entries.shape
    spot = [jax.random.randint(jax.random.fold_in(rng, axis), (), 0, extent[axis]) for axis in range(len(extent))]
    entries = entries.at[tuple(spot)].set(least)
    longest = extent.index(max(extent))
    spot[longest] = (spot[longest] + 1) % extent[longest]
    return entries.at[tuple(spot)].set(top_value)


def block_levels(key, extent, pieces, low, largest):
    level, own = 1.0, jax.random.fold_in(key, 6)
    for axis_at, parts in pieces:
        draws = jnp.exp(jax.random.uniform(jax.random.fold_in(own, axis_at), (parts,), jnp.float32, low / len(pieces), largest / len(pieces)))
        level = level * jnp.repeat(draws, extent[axis_at] // parts).reshape([-1 if axis == axis_at else 1 for axis in range(len(extent))])
    return level


def gaussian(own_key, shape, scale, limit, cuts=(), kind=jnp.bfloat16):
    values = scale * jax.random.normal(own_key, shape, jnp.float32)
    if cuts:
        values = values * block_levels(own_key, shape, cuts, -0.22, 0.18)
    return jnp.clip(values, -limit, limit).astype(kind)


def setup_inputs(seed: int = 0) -> dict:
    keys = jax.random.split(jax.random.key(seed), 7)
    return {
        "stiff_rows": gaussian(keys[0], (FINE, SLOTS, NB, NB), 0.125, 0.75, ((0, 512),)),
        "stiff_iface": gaussian(keys[1], (FINE, 2, NB, NB), 0.125, 0.75, ((0, 512),)),
        "columns": draw_columns(jax.random.fold_in(keys[6], 71), 0),
        "live_count": touch_ends(jax.random.randint(keys[3], (FINE,), 2, SLOTS + 1), jax.random.fold_in(keys[3], 1), 2, SLOTS).astype(jnp.int32),
        "aggregate": touch_ends(jax.random.randint(keys[4], (FINE,), 0, COARSE), jax.random.fold_in(keys[4], 1), 0, COARSE - 1).astype(jnp.int32),
        "prolong": gaussian(keys[5], (FINE, NB, NB), NB ** -0.5, 0.3125, ((0, 512),)),
    }


def reference(stiff_rows, stiff_iface, columns, live_count, aggregate, prolong):
    width = 3 * COARSE * NB
    start_band = jnp.zeros((CROWS, width), jnp.float32)
    sides = jnp.concatenate([jnp.ones((SLOTS,), jnp.int32), jnp.array([0, 2], jnp.int32)])

    def one_row(band, index):
        group_at = index // N_DEV
        coupled = (group_at * N_DEV + columns[index]).astype(jnp.int32)
        lower_row = jnp.maximum(index - N_DEV, 0).astype(jnp.int32)
        upper_row = jnp.minimum(index + N_DEV, FINE - 1).astype(jnp.int32)
        blocks = jnp.concatenate([prolong[coupled], prolong[lower_row][None], prolong[upper_row][None]], axis=0)
        stiff = jnp.concatenate([stiff_rows[index], stiff_iface[index]], axis=0)
        qmat = jnp.einsum("kfg,kgm->kfm", stiff.astype(jnp.float32), blocks.astype(jnp.float32)).astype(jnp.bfloat16)
        contrib = jnp.einsum("fc,kfm->kcm", prolong[index].astype(jnp.float32), qmat.astype(jnp.float32))
        targets = jnp.concatenate([aggregate[coupled], aggregate[lower_row][None], aggregate[upper_row][None]])
        weights = jnp.concatenate([
            (jnp.arange(SLOTS, dtype=jnp.int32) < live_count[index]).astype(jnp.float32),
            (group_at > 0).astype(jnp.float32)[None],
            (group_at < N_GRP - 1).astype(jnp.float32)[None]])
        side_hot = (sides[:, None] == jnp.arange(3, dtype=jnp.int32)[None, :]).astype(jnp.float32)
        block_hot = (targets[:, None] == jnp.arange(COARSE, dtype=jnp.int32)[None, :]).astype(jnp.float32)
        placing = side_hot[:, :, None] * block_hot[:, None, :] * weights[:, None, None]
        partial_value = jnp.einsum("ksb,kcm->csbm", placing, contrib).reshape(NB, width)
        partial_value = lax.optimization_barrier(partial_value.astype(jnp.bfloat16)).astype(jnp.float32)
        row_start = ((group_at * COARSE + aggregate[index]) * NB).astype(jnp.int32)
        zero_col = jnp.zeros((), jnp.int32)
        current = lax.dynamic_slice(band, (row_start, zero_col), (NB, width))
        band = lax.dynamic_update_slice(band, current + partial_value, (row_start, zero_col))
        return band, None

    band, _ = lax.scan(one_row, start_band, jnp.arange(FINE, dtype=jnp.int32))
    return band
```

```python
import jax
import jax.numpy as jnp
from jax import lax
from jax.experimental import pallas as pl
from jax.experimental.pallas import tpu as pltpu
from jax.sharding import PartitionSpec as P

NB = 384
SLOTS = 6
TAIL = 16
ROWS = NB + TAIL
CUT = 192
SIDE = 4
BAND = 48
HALF = 3 * NB
MESH = pl.DeviceIdType.MESH
BF = jnp.bfloat16
F32 = jnp.float32


def kernel(
    cols, live, agg, stiff_rows, stiff_iface, prolong, out,
    win, bbuf, pt, tbuf, acc, xbuf, pbuf, dense, got_far, got_near, gather, got_last, fin, got_fin,
    load_sem, send_sem, recv_sem, send2, recv2,
):
    g = lax.axis_index("grp")
    d = lax.axis_index("dev")
    groups = lax.axis_size("grp")
    devs = lax.axis_size("dev")
    k = lax.rem(d, 2)
    c = d // 2
    chips = devs // 2
    x = c // SIDE
    y = lax.rem(c, SIDE)
    own = 2 + k

    def at(cx, cy, core):
        return (g, (lax.rem(cx, SIDE) * SIDE + lax.rem(cy, SIDE)) * 2 + core)

    partner = (g, c * 2 + 1 - k)
    nxt = (g, lax.rem(c + 1, chips) * 2 + k)
    prv = (g, lax.rem(c + chips - 1, chips) * 2 + k)
    far = (g, lax.rem(c + chips + 2 * k - 1, chips) * 2 + 1 - k)
    above = (lax.rem(g + 1, groups), d)
    below = (lax.rem(g + groups - 1, groups), d)
    fx, fy = 1 - k, k
    first_up = at(x + fx, y + fy, k)
    first_down = at(x + 3 * fx, y + 3 * fy, k)
    second = [at(x + s * fy, y + s * fx, k) for s in (1, 2, 3)]

    load_p = pltpu.make_async_copy(prolong.at[0], win.at[own, pl.ds(0, NB)], load_sem.at[0])
    load_b = pltpu.make_async_copy(stiff_rows.at[0], bbuf.at[pl.ds(0, SLOTS)], load_sem.at[1])
    load_i = pltpu.make_async_copy(stiff_iface.at[0], bbuf.at[pl.ds(SLOTS, 2)], load_sem.at[2])
    load_p.start()
    win[own, NB:ROWS, :] = jnp.full((TAIL, NB), agg[0].astype(F32), F32).astype(BF)

    barrier = pltpu.get_barrier_semaphore()
    peers = [partner, nxt, prv, far, above, below, first_up, first_down] + second
    for peer in peers:
        pl.semaphore_signal(barrier, inc=1, device_id=peer, device_id_type=MESH)
    load_p.wait()
    load_b.start()
    load_i.start()
    pl.semaphore_wait(barrier, len(peers))

    parts = (pl.ds(0, CUT), pl.ds(CUT, ROWS - CUT))

    def remote(src, dst, sems, rems, peer):
        return pltpu.make_async_remote_copy(
            src_ref=src, dst_ref=dst, send_sem=sems, recv_sem=rems, device_id=peer, device_id_type=MESH
        )

    sent = []

    def go(copy):
        copy.start()
        sent.append(copy)

    def move(src_slot, dst_slot, part, number, peer):
        return remote(
            win.at[src_slot, parts[part]], win.at[dst_slot, parts[part]],
            send_sem.at[number], recv_sem.at[dst_slot, part], peer,
        )

    def arrived(slot, part):
        move(slot, slot, part, 0, partner).wait_recv()

    for part in range(2):
        go(move(own, k, part, part, nxt))
        go(move(own, 4 + k, part, 2 + part, prv))
    for part in range(2):
        go(move(own, 7, part, 4 + part, above))
        go(move(own, 8, part, 6 + part, below))
        go(move(own, own, part, 8 + part, partner))

    pt[...] = win[own, 0:NB, :].astype(F32).T.astype(BF)
    load_b.wait()
    load_i.wait()

    @pl.loop(0, SLOTS + 2)
    def _(index):
        tbuf[index] = jnp.dot(pt[...], bbuf[index], preferred_element_type=F32).astype(BF)

    base = 2 * c
    live_now = live[0]
    slot_of = []
    for index in range(SLOTS):
        rel = lax.rem(cols[0, index] - base + 2 + 2 * devs, devs)
        slot_of.append(jnp.minimum(rel, 6))

    def row_of(slot):
        return win[slot, NB:ROWS, :].astype(F32)[0:1, :]

    def take_in(slot, fresh=False):
        index = jnp.int32(0)
        weight = jnp.int32(0)
        for number in range(SLOTS):
            hit = (slot_of[number] == slot).astype(jnp.int32)
            index = index + hit * number
            weight = weight + hit * (number < live_now).astype(jnp.int32)
        index = jnp.minimum(index, SLOTS - 1)
        scale = weight.astype(F32)
        high = row_of(slot) * scale
        low = scale - high
        value = jnp.dot(tbuf[index], win[slot, 0:NB, :], preferred_element_type=F32)
        if fresh:
            acc[1] = value * low
            acc[2] = value * high
        else:
            acc[1] += value * low
            acc[2] += value * high

    take_in(own, True)
    for part in range(2):
        arrived(3 - k, part)
    take_in(3 - k)

    relay_from = 4 - 3 * k
    for part in range(2):
        arrived(k, part)
        arrived(4 + k, part)
        go(move(relay_from, 6, part, 10 + part, far))
        go(move(k, k, part, 12 + part, partner))
        go(move(4 + k, 4 + k, part, 14 + part, partner))
    take_in(k)
    take_in(4 + k)

    for slot, index, place, weight in (
        (7, SLOTS, 0, (g > 0).astype(F32)),
        (8, SLOTS + 1, 3, (g < groups - 1).astype(F32)),
    ):
        for part in range(2):
            arrived(slot, part)
        value = jnp.dot(tbuf[index], win[slot, 0:NB, :], preferred_element_type=F32) * weight
        acc[place] = value
        xbuf[place, 0:NB, :] = value.astype(BF)
        xbuf[place, NB:ROWS, :] = win[slot, NB:ROWS, :]

    for slot in (1 - k, 5 - k, 6):
        for part in range(2):
            arrived(slot, part)
        take_in(slot)

    for place in (1, 2):
        xbuf[place, 0:NB, :] = acc[place].astype(BF)
        xbuf[place, NB:ROWS, :] = jnp.zeros((TAIL, NB), BF)

    def second_copy(src, dst, number, peer):
        return remote(src, dst, send2.at[number], recv2.at[number], peer)

    pair = second_copy(xbuf.at[pl.ds(2 * (1 - k), 2)], pbuf, 0, partner)
    go(pair)
    pair.wait_recv()

    edge_mine, mid_mine = 3 * k, 1 + k
    edge_theirs, mid_theirs = k, 1 - k
    mine_row = row_of(own)
    their_row = row_of(3 - k)
    edge_row = xbuf[edge_mine, NB:ROWS, :].astype(F32)[0:1, :]
    edge_row2 = pbuf[edge_theirs, NB:ROWS, :].astype(F32)[0:1, :]

    @pl.loop(0, 2 * SIDE)
    def _(block):
        rows = pl.ds(pl.multiple_of(block * BAND, BAND), BAND)
        e1 = acc[edge_mine, rows, :]
        m1 = acc[mid_mine, rows, :]
        e2 = pbuf[edge_theirs, rows, :].astype(F32)
        m2 = pbuf[mid_theirs, rows, :].astype(F32)
        for coarse in range(2):
            w1 = mine_row if coarse else 1.0 - mine_row
            w2 = their_row if coarse else 1.0 - their_row
            to_x = 2 * coarse + block // SIDE
            to_y = lax.rem(block, SIDE)
            u = to_x * fx + to_y * fy
            v = to_x * fy + to_y * fx
            dense[u, v, :, 0:NB] = (e1 * (w1 * (1.0 - edge_row)) + e2 * (w2 * (1.0 - edge_row2))).astype(BF)
            dense[u, v, :, NB:2 * NB] = (e1 * (w1 * edge_row) + e2 * (w2 * edge_row2)).astype(BF)
            dense[u, v, :, 2 * NB:HALF] = (m1 * w1 + m2 * w2).astype(BF)

    me = x * fx + y * fy
    up = lax.rem(me + 1, SIDE)
    opposite = lax.rem(me + 2, SIDE)
    down = lax.rem(me + 3, SIDE)
    lo, hi = pl.ds(0, 2), pl.ds(2, 2)
    far_up = second_copy(dense.at[opposite, lo], got_far.at[0], 1, first_up)
    far_down = second_copy(dense.at[opposite, hi], got_far.at[1], 2, first_down)
    go(far_up)
    go(far_down)
    up_hi = second_copy(dense.at[up, hi], got_near.at[0, hi], 3, first_up)
    down_lo = second_copy(dense.at[down, lo], got_near.at[1, lo], 4, first_down)
    go(up_hi)
    go(down_lo)
    far_up.wait_recv()
    for v in range(2):
        dense[up, v] = (dense[up, v].astype(F32) + got_far[0, v].astype(F32)).astype(BF)
    up_lo = second_copy(dense.at[up, lo], got_near.at[0, lo], 5, first_up)
    go(up_lo)
    far_down.wait_recv()
    for v in range(2):
        dense[down, 2 + v] = (dense[down, 2 + v].astype(F32) + got_far[1, v].astype(F32)).astype(BF)
    down_hi = second_copy(dense.at[down, hi], got_near.at[1, hi], 6, first_down)
    go(down_hi)
    for copy in (up_hi, down_lo, up_lo, down_hi):
        copy.wait_recv()

    @pl.loop(0, SIDE)
    def _(v):
        gather[v] = (
            dense[me, v].astype(F32) + got_near[0, v].astype(F32) + got_near[1, v].astype(F32)
        ).astype(BF)

    mine = x * fy + y * fx
    lasts = []
    for step in (2, 1, 3):
        copy = second_copy(
            gather.at[lax.rem(mine + step, SIDE)], got_last.at[step - 1], 6 + step, second[step - 1]
        )
        go(copy)
        lasts.append(copy)
    for copy in lasts:
        copy.wait_recv()
    fin[...] = (
        gather[mine].astype(F32) + got_last[0].astype(F32) + got_last[1].astype(F32) + got_last[2].astype(F32)
    ).reshape(2, BAND // 2, HALF)

    swap = second_copy(fin.at[1 - k], got_fin, 10, partner)
    go(swap)

    def place_half(side, ref):
        edge_at = side * (HALF + NB)
        mid_at = 2 * NB + side * NB
        out[:, pl.ds(pl.multiple_of(edge_at, 128), 2 * NB)] = ref[:, 0:2 * NB]
        out[:, pl.ds(pl.multiple_of(mid_at, 128), NB)] = ref[:, 2 * NB:HALF]

    place_half(k, fin.at[k])
    swap.wait_recv()
    place_half(1 - k, got_fin)
    for copy in sent:
        copy.wait_send()


def on_device(stiff_rows, stiff_iface, columns, live_count, aggregate, prolong):
    smem = pl.BlockSpec(memory_space=pltpu.SMEM)
    anywhere = pl.BlockSpec(memory_space=pl.ANY)
    return pl.pallas_call(
        kernel,
        out_shape=jax.ShapeDtypeStruct((BAND // 2, 2 * HALF), F32),
        in_specs=[smem, smem, smem, anywhere, anywhere, anywhere],
        out_specs=pl.BlockSpec(memory_space=pltpu.VMEM),
        scratch_shapes=[
            pltpu.VMEM((9, ROWS, NB), BF),
            pltpu.VMEM((SLOTS + 2, NB, NB), BF),
            pltpu.VMEM((NB, NB), BF),
            pltpu.VMEM((SLOTS + 2, NB, NB), BF),
            pltpu.VMEM((4, NB, NB), F32),
            pltpu.VMEM((4, ROWS, NB), BF),
            pltpu.VMEM((2, ROWS, NB), BF),
            pltpu.VMEM((SIDE, SIDE, BAND, HALF), BF),
            pltpu.VMEM((2, 2, BAND, HALF), BF),
            pltpu.VMEM((2, SIDE, BAND, HALF), BF),
            pltpu.VMEM((SIDE, BAND, HALF), BF),
            pltpu.VMEM((3, BAND, HALF), BF),
            pltpu.VMEM((2, BAND // 2, HALF), F32),
            pltpu.VMEM((BAND // 2, HALF), F32),
            pltpu.SemaphoreType.DMA((3,)),
            pltpu.SemaphoreType.DMA((16,)),
            pltpu.SemaphoreType.DMA((9, 2)),
            pltpu.SemaphoreType.DMA((11,)),
            pltpu.SemaphoreType.DMA((11,)),
        ],
        compiler_params=pltpu.CompilerParams(
            collective_id=0, has_side_effects=True, vmem_limit_bytes=60 * 1024 * 1024
        ),
        name="coarse",
    )(columns, live_count, aggregate, stiff_rows, stiff_iface, prolong)


def solution(mesh):
    in_specs = (
        P(("grp", "dev"), None, None, None),
        P(("grp", "dev"), None, None, None),
        P(("grp", "dev"), None),
        P(("grp", "dev")),
        P(("grp", "dev")),
        P(("grp", "dev"), None, None),
    )
    out_specs = P(("grp", "dev"), None)
    return jax.shard_map(
        on_device, mesh=mesh, in_specs=in_specs, out_specs=out_specs, check_vma=False
    )
```

```python
import jax
import jax.numpy as jnp
from jax import lax
from jax.experimental import pallas as pl
from jax.experimental.pallas import tpu as pltpu
from jax.sharding import PartitionSpec as P

NB = 384
SLOTS = 6
TAIL = 16
ROWS = NB + TAIL
CUT = 192
SIDE = 4
BAND = 48
HALF = 3 * NB
MESH = pl.DeviceIdType.MESH
BF = jnp.bfloat16
F32 = jnp.float32


def kernel(
    cols, live, agg, stiff_rows, stiff_iface, prolong, out,
    win, bbuf, pt, tbuf, acc, acc_e, xe, pe, xm, pm,
    dense_e, far_e, near_e, sum_e, last_e, dense_m, far_m, near_m, sum_m, last_m, fin, got_fin,
    load_sem, send_sem, recv_sem, send2, recv2,
):
    g = lax.axis_index("grp")
    d = lax.axis_index("dev")
    groups = lax.axis_size("grp")
    devs = lax.axis_size("dev")
    k = lax.rem(d, 2)
    c = d // 2
    chips = devs // 2
    x = c // SIDE
    y = lax.rem(c, SIDE)
    own = 2 + k

    def at(cx, cy):
        return (g, (lax.rem(cx, SIDE) * SIDE + lax.rem(cy, SIDE)) * 2 + k)

    partner = (g, c * 2 + 1 - k)
    nxt = (g, lax.rem(c + 1, chips) * 2 + k)
    prv = (g, lax.rem(c + chips - 1, chips) * 2 + k)
    far = (g, lax.rem(c + chips + 2 * k - 1, chips) * 2 + 1 - k)
    above = (jnp.minimum(g + 1, groups - 1), d)
    below = (jnp.maximum(g - 1, 0), d)
    has_above = g < groups - 1
    has_below = g > 0
    along_x = [at(x + s, y) for s in (1, 2, 3)]
    along_y = [at(x, y + s) for s in (1, 2, 3)]

    load_p = pltpu.make_async_copy(prolong.at[0], win.at[own, pl.ds(0, NB)], load_sem.at[0])
    load_b = pltpu.make_async_copy(stiff_rows.at[0], bbuf.at[pl.ds(0, SLOTS)], load_sem.at[1])
    load_i = pltpu.make_async_copy(stiff_iface.at[0], bbuf.at[pl.ds(SLOTS, 2)], load_sem.at[2])
    load_p.start()

    barrier = pltpu.get_barrier_semaphore()
    peers = [partner, nxt, prv, far] + along_x + along_y

    @pl.when(has_above)
    def _():
        pl.semaphore_signal(barrier, inc=1, device_id=above, device_id_type=MESH)

    @pl.when(has_below)
    def _():
        pl.semaphore_signal(barrier, inc=1, device_id=below, device_id_type=MESH)

    for peer in peers:
        pl.semaphore_signal(barrier, inc=1, device_id=peer, device_id_type=MESH)
    win[own, NB:ROWS, :] = jnp.full((TAIL, NB), agg[0].astype(F32), F32).astype(BF)

    @pl.when(jnp.logical_not(has_below))
    def _():
        win[7] = jnp.zeros((ROWS, NB), BF)

    @pl.when(jnp.logical_not(has_above))
    def _():
        win[8] = jnp.zeros((ROWS, NB), BF)

    load_p.wait()
    load_b.start()
    load_i.start()
    pl.semaphore_wait(barrier, len(peers) + has_above.astype(jnp.int32) + has_below.astype(jnp.int32))

    parts = (pl.ds(0, CUT), pl.ds(CUT, ROWS - CUT))

    def remote(src, dst, sems, rems, peer):
        return pltpu.make_async_remote_copy(
            src_ref=src, dst_ref=dst, send_sem=sems, recv_sem=rems, device_id=peer, device_id_type=MESH
        )

    sent = []

    def go(copy):
        copy.start()
        sent.append(copy)
        return copy

    def move(src_slot, dst_slot, part, number, peer):
        return remote(
            win.at[src_slot, parts[part]], win.at[dst_slot, parts[part]],
            send_sem.at[number], recv_sem.at[dst_slot, part], peer,
        )

    def arrived(slot, part):
        move(slot, slot, part, 0, partner).wait_recv()

    to_above = remote(win.at[own], win.at[7], send_sem.at[4], recv_sem.at[7, 0], above)
    to_below = remote(win.at[own], win.at[8], send_sem.at[5], recv_sem.at[8, 0], below)
    for part in range(2):
        go(move(own, k, part, part, nxt))
        go(move(own, 4 + k, part, 2 + part, prv))

    @pl.when(has_above)
    def _():
        to_above.start()

    @pl.when(has_below)
    def _():
        to_below.start()

    for part in range(2):
        go(move(own, own, part, 8 + part, partner))

    pt[...] = win[own, 0:NB, :].astype(F32).T.astype(BF)
    load_b.wait()
    load_i.wait()

    @pl.loop(0, SLOTS + 2)
    def _(index):
        tbuf[index] = jnp.dot(pt[...], bbuf[index], preferred_element_type=F32).astype(BF)

    base = 2 * c
    live_now = live[0]
    slot_of = []
    for index in range(SLOTS):
        rel = lax.rem(cols[0, index] - base + 2 + 2 * devs, devs)
        slot_of.append(jnp.minimum(rel, 6))

    def row_of(slot):
        return win[slot, NB:ROWS, :].astype(F32)[0:1, :]

    def take_in(slot, fresh=False):
        index = jnp.int32(0)
        weight = jnp.int32(0)
        for number in range(SLOTS):
            hit = (slot_of[number] == slot).astype(jnp.int32)
            index = index + hit * number
            weight = weight + hit * (number < live_now).astype(jnp.int32)
        index = jnp.minimum(index, SLOTS - 1)
        scale = weight.astype(F32)
        high = row_of(slot) * scale
        low = scale - high
        value = jnp.dot(tbuf[index], win[slot, 0:NB, :], preferred_element_type=F32)
        if fresh:
            acc[0] = value * low
            acc[1] = value * high
        else:
            acc[0] += value * low
            acc[1] += value * high

    take_in(own, True)
    for part in range(2):
        arrived(3 - k, part)
    take_in(3 - k)

    relay_from = 4 - 3 * k
    for part in range(2):
        arrived(relay_from, part)
        go(move(relay_from, 6, part, 10 + part, far))
        arrived(5 * k, part)
        go(move(k, k, part, 12 + part, partner))
        go(move(4 + k, 4 + k, part, 14 + part, partner))

    @pl.when(has_below)
    def _():
        to_above.wait_recv()

    @pl.when(has_above)
    def _():
        to_below.wait_recv()

    def second_copy(src, dst, number, peer):
        return remote(src, dst, send2.at[number], recv2.at[number], peer)

    xe[0:NB, :] = jnp.dot(tbuf[7 - k], win[8 - k, 0:NB, :], preferred_element_type=F32).astype(BF)
    xe[NB:ROWS, :] = win[8 - k, NB:ROWS, :]
    pair_e = go(second_copy(xe, pe, 0, partner))
    acc_e[...] = jnp.dot(tbuf[6 + k], win[7 + k, 0:NB, :], preferred_element_type=F32)
    mine_row = row_of(own)
    their_row = row_of(3 - k)
    edge_row = row_of(7 + k)
    pair_e.wait_recv()
    edge_row2 = pe[NB:ROWS, :].astype(F32)[0:1, :]

    @pl.loop(0, 2 * SIDE)
    def _(block):
        rows = pl.ds(pl.multiple_of(block * BAND, BAND), BAND)
        e1 = acc_e[rows, :]
        e2 = pe[rows, :].astype(F32)
        for coarse in range(2):
            w1 = mine_row if coarse else 1.0 - mine_row
            w2 = their_row if coarse else 1.0 - their_row
            u = 2 * coarse + block // SIDE
            v = lax.rem(block, SIDE)
            dense_e[u, v, :, 0:NB] = (e1 * (w1 * (1.0 - edge_row)) + e2 * (w2 * (1.0 - edge_row2))).astype(BF)
            dense_e[u, v, :, NB:2 * NB] = (e1 * (w1 * edge_row) + e2 * (w2 * edge_row2)).astype(BF)

    lo, hi = pl.ds(0, 2), pl.ds(2, 2)

    class Ring:
        def __init__(self, buf, far_buf, near_buf, total, me, line, number):
            self.buf, self.far, self.near, self.total, self.me = buf, far_buf, near_buf, total, me
            self.plus, self.minus, self.number = line[0], line[2], number
            self.up = lax.rem(me + 1, SIDE)
            self.opposite = lax.rem(me + 2, SIDE)
            self.down = lax.rem(me + 3, SIDE)

        def begin(self):
            n, buf = self.number, self.buf
            self.first = [
                go(second_copy(buf.at[self.opposite, lo], self.far.at[0], n, self.plus)),
                go(second_copy(buf.at[self.opposite, hi], self.far.at[1], n + 1, self.minus)),
            ]
            self.rest = [
                go(second_copy(buf.at[self.up, hi], self.near.at[0, hi], n + 2, self.plus)),
                go(second_copy(buf.at[self.down, lo], self.near.at[1, lo], n + 3, self.minus)),
            ]

        def relay(self):
            n, buf = self.number, self.buf
            self.first[0].wait_recv()
            for v in range(2):
                buf[self.up, v] = (buf[self.up, v].astype(F32) + self.far[0, v].astype(F32)).astype(BF)
            self.rest.append(go(second_copy(buf.at[self.up, lo], self.near.at[0, lo], n + 4, self.plus)))
            self.first[1].wait_recv()
            for v in range(2):
                buf[self.down, 2 + v] = (
                    buf[self.down, 2 + v].astype(F32) + self.far[1, v].astype(F32)
                ).astype(BF)
            self.rest.append(go(second_copy(buf.at[self.down, hi], self.near.at[1, hi], n + 5, self.minus)))

        def end(self):
            for copy in self.rest:
                copy.wait_recv()

            @pl.loop(0, SIDE)
            def _(v):
                self.total[v] = (
                    self.buf[self.me, v].astype(F32) + self.near[0, v].astype(F32) + self.near[1, v].astype(F32)
                ).astype(BF)

    ring_e = Ring(dense_e, far_e, near_e, sum_e, x, along_x, 2)
    ring_m = Ring(dense_m, far_m, near_m, sum_m, y, along_y, 8)
    ring_e.begin()

    take_in(k)
    take_in(4 + k)
    for slot in (1 - k, 5 - k, 6):
        for part in range(2):
            arrived(slot, part)
        take_in(slot)
    xm[...] = acc[1 - k].astype(BF)
    pair_m = go(second_copy(xm, pm, 1, partner))
    ring_e.relay()
    pair_m.wait_recv()

    @pl.loop(0, 2 * SIDE)
    def _(block):
        rows = pl.ds(pl.multiple_of(block * BAND, BAND), BAND)
        m1 = acc[k, rows, :]
        m2 = pm[rows, :].astype(F32)
        for coarse in range(2):
            w1 = mine_row if coarse else 1.0 - mine_row
            w2 = their_row if coarse else 1.0 - their_row
            dense_m[lax.rem(block, SIDE), 2 * coarse + block // SIDE] = (m1 * w1 + m2 * w2).astype(BF)

    ring_m.begin()

    def spread(total, last, me, line, number):
        return [
            go(second_copy(total.at[lax.rem(me + step, SIDE)], last.at[step - 1], number + step, line[step - 1]))
            for step in (2, 1, 3)
        ]

    ring_e.end()
    lasts = spread(sum_e, last_e, y, along_y, 13)
    ring_m.relay()
    ring_m.end()
    lasts = lasts + spread(sum_m, last_m, x, along_x, 16)
    for copy in lasts:
        copy.wait_recv()

    def closed(total, last, me, width):
        value = total[me].astype(F32)
        for number in range(3):
            value = value + last[number].astype(F32)
        return value.reshape(2, BAND // 2, width)

    fin[:, :, 0:2 * NB] = closed(sum_e, last_e, y, 2 * NB)
    fin[:, :, 2 * NB:HALF] = closed(sum_m, last_m, x, NB)
    swap = go(second_copy(fin.at[1 - k], got_fin, 20, partner))

    def place_half(side, ref):
        edge_at = side * (HALF + NB)
        mid_at = 2 * NB + side * NB
        out[:, pl.ds(pl.multiple_of(edge_at, 128), 2 * NB)] = ref[:, 0:2 * NB]
        out[:, pl.ds(pl.multiple_of(mid_at, 128), NB)] = ref[:, 2 * NB:HALF]

    place_half(k, fin.at[k])
    swap.wait_recv()
    place_half(1 - k, got_fin)

    @pl.when(has_above)
    def _():
        to_above.wait_send()

    @pl.when(has_below)
    def _():
        to_below.wait_send()

    for copy in sent:
        copy.wait_send()


def ring_buffers(width):
    return [
        pltpu.VMEM((SIDE, SIDE, BAND, width), BF),
        pltpu.VMEM((2, 2, BAND, width), BF),
        pltpu.VMEM((2, SIDE, BAND, width), BF),
        pltpu.VMEM((SIDE, BAND, width), BF),
        pltpu.VMEM((3, BAND, width), BF),
    ]


def on_device(stiff_rows, stiff_iface, columns, live_count, aggregate, prolong):
    smem = pl.BlockSpec(memory_space=pltpu.SMEM)
    anywhere = pl.BlockSpec(memory_space=pl.ANY)
    return pl.pallas_call(
        kernel,
        out_shape=jax.ShapeDtypeStruct((BAND // 2, 2 * HALF), F32),
        in_specs=[smem, smem, smem, anywhere, anywhere, anywhere],
        out_specs=pl.BlockSpec(memory_space=pltpu.VMEM),
        scratch_shapes=[
            pltpu.VMEM((9, ROWS, NB), BF),
            pltpu.VMEM((SLOTS + 2, NB, NB), BF),
            pltpu.VMEM((NB, NB), BF),
            pltpu.VMEM((SLOTS + 2, NB, NB), BF),
            pltpu.VMEM((2, NB, NB), F32),
            pltpu.VMEM((NB, NB), F32),
            pltpu.VMEM((ROWS, NB), BF),
            pltpu.VMEM((ROWS, NB), BF),
            pltpu.VMEM((NB, NB), BF),
            pltpu.VMEM((NB, NB), BF),
            *ring_buffers(2 * NB),
            *ring_buffers(NB),
            pltpu.VMEM((2, BAND // 2, HALF), F32),
            pltpu.VMEM((BAND // 2, HALF), F32),
            pltpu.SemaphoreType.DMA((3,)),
            pltpu.SemaphoreType.DMA((16,)),
            pltpu.SemaphoreType.DMA((9, 2)),
            pltpu.SemaphoreType.DMA((21,)),
            pltpu.SemaphoreType.DMA((21,)),
        ],
        compiler_params=pltpu.CompilerParams(
            collective_id=0, has_side_effects=True, vmem_limit_bytes=60 * 1024 * 1024
        ),
        name="coarse",
    )(columns, live_count, aggregate, stiff_rows, stiff_iface, prolong)


def solution(mesh):
    in_specs = (
        P(("grp", "dev"), None, None, None),
        P(("grp", "dev"), None, None, None),
        P(("grp", "dev"), None),
        P(("grp", "dev")),
        P(("grp", "dev")),
        P(("grp", "dev"), None, None),
    )
    out_specs = P(("grp", "dev"), None)
    return jax.shard_map(
        on_device, mesh=mesh, in_specs=in_specs, out_specs=out_specs, check_vma=False
    )
```

```python
import jax
import jax.numpy as jnp
from jax import lax
from jax.experimental import pallas as pl
from jax.experimental.pallas import tpu as pltpu
from jax.sharding import PartitionSpec as P

NB = 384
SLOTS = 6
TAIL = 16
ROWS = NB + TAIL
CUT = 192
SIDE = 4
BAND = 48
HALF = 3 * NB
MESH = pl.DeviceIdType.MESH
BF = jnp.bfloat16
F32 = jnp.float32


def kernel(
    cols, live, agg, stiff_rows, stiff_iface, prolong, out,
    win, bbuf, pt, tbuf, acc, acc_e, xe, pe, xm, pm,
    dense_e, far_e, near_e, sum_e, last_e, dense_m, far_m, near_m, sum_m, last_m, fin, got_fin,
    load_sem, send_sem, recv_sem, send2, recv2,
):
    g = lax.axis_index("grp")
    d = lax.axis_index("dev")
    groups = lax.axis_size("grp")
    devs = lax.axis_size("dev")
    k = lax.rem(d, 2)
    c = d // 2
    chips = devs // 2
    x = c // SIDE
    y = lax.rem(c, SIDE)
    own = 2 + k

    fx, fy = 1 - k, k

    def at(cx, cy):
        return (g, (lax.rem(cx, SIDE) * SIDE + lax.rem(cy, SIDE)) * 2 + k)

    partner = (g, c * 2 + 1 - k)
    nxt = (g, lax.rem(c + 1, chips) * 2 + k)
    prv = (g, lax.rem(c + chips - 1, chips) * 2 + k)
    far = (g, lax.rem(c + chips + 2 * k - 1, chips) * 2 + 1 - k)
    above = (jnp.minimum(g + 1, groups - 1), d)
    below = (jnp.maximum(g - 1, 0), d)
    has_above = g < groups - 1
    has_below = g > 0
    first_at = x * fx + y * fy
    second_at = x * fy + y * fx
    first_line = [at(x + s * fx, y + s * fy) for s in (1, 2, 3)]
    second_line = [at(x + s * fy, y + s * fx) for s in (1, 2, 3)]

    load_p = pltpu.make_async_copy(prolong.at[0], win.at[own, pl.ds(0, NB)], load_sem.at[0])
    load_b = pltpu.make_async_copy(stiff_rows.at[0], bbuf.at[pl.ds(0, SLOTS)], load_sem.at[1])
    load_i = pltpu.make_async_copy(stiff_iface.at[0], bbuf.at[pl.ds(SLOTS, 2)], load_sem.at[2])
    load_p.start()

    barrier = pltpu.get_barrier_semaphore()
    peers = [partner, nxt, prv, far] + first_line + second_line

    @pl.when(has_above)
    def _():
        pl.semaphore_signal(barrier, inc=1, device_id=above, device_id_type=MESH)

    @pl.when(has_below)
    def _():
        pl.semaphore_signal(barrier, inc=1, device_id=below, device_id_type=MESH)

    for peer in peers:
        pl.semaphore_signal(barrier, inc=1, device_id=peer, device_id_type=MESH)
    win[own, NB:ROWS, :] = jnp.full((TAIL, NB), agg[0].astype(F32), F32).astype(BF)

    @pl.when(jnp.logical_not(has_below))
    def _():
        win[7] = jnp.zeros((ROWS, NB), BF)

    @pl.when(jnp.logical_not(has_above))
    def _():
        win[8] = jnp.zeros((ROWS, NB), BF)

    load_p.wait()
    load_b.start()
    load_i.start()
    pl.semaphore_wait(barrier, len(peers) + has_above.astype(jnp.int32) + has_below.astype(jnp.int32))

    parts = (pl.ds(0, CUT), pl.ds(CUT, ROWS - CUT))

    def remote(src, dst, sems, rems, peer):
        return pltpu.make_async_remote_copy(
            src_ref=src, dst_ref=dst, send_sem=sems, recv_sem=rems, device_id=peer, device_id_type=MESH
        )

    sent = []

    def go(copy):
        copy.start()
        sent.append(copy)
        return copy

    def move(src_slot, dst_slot, part, number, peer):
        return remote(
            win.at[src_slot, parts[part]], win.at[dst_slot, parts[part]],
            send_sem.at[number], recv_sem.at[dst_slot, part], peer,
        )

    def arrived(slot, part):
        move(slot, slot, part, 0, partner).wait_recv()

    to_above = remote(win.at[own], win.at[7], send_sem.at[4], recv_sem.at[7, 0], above)
    to_below = remote(win.at[own], win.at[8], send_sem.at[5], recv_sem.at[8, 0], below)
    for part in range(2):
        go(move(own, k, part, part, nxt))
        go(move(own, 4 + k, part, 2 + part, prv))

    @pl.when(has_above)
    def _():
        to_above.start()

    @pl.when(has_below)
    def _():
        to_below.start()

    for part in range(2):
        go(move(own, own, part, 8 + part, partner))

    pt[...] = win[own, 0:NB, :].astype(F32).T.astype(BF)
    load_b.wait()
    load_i.wait()

    @pl.loop(0, SLOTS + 2)
    def _(index):
        tbuf[index] = jnp.dot(pt[...], bbuf[index], preferred_element_type=F32).astype(BF)

    base = 2 * c
    live_now = live[0]
    slot_of = []
    for index in range(SLOTS):
        rel = lax.rem(cols[0, index] - base + 2 + 2 * devs, devs)
        slot_of.append(jnp.minimum(rel, 6))

    def row_of(slot):
        return win[slot, NB:ROWS, :].astype(F32)[0:1, :]

    def take_in(slot, fresh=False):
        index = jnp.int32(0)
        weight = jnp.int32(0)
        for number in range(SLOTS):
            hit = (slot_of[number] == slot).astype(jnp.int32)
            index = index + hit * number
            weight = weight + hit * (number < live_now).astype(jnp.int32)
        index = jnp.minimum(index, SLOTS - 1)
        scale = weight.astype(F32)
        high = row_of(slot) * scale
        low = scale - high
        value = jnp.dot(tbuf[index], win[slot, 0:NB, :], preferred_element_type=F32)
        if fresh:
            acc[0] = value * low
            acc[1] = value * high
        else:
            acc[0] += value * low
            acc[1] += value * high

    take_in(own, True)
    for part in range(2):
        arrived(3 - k, part)
    take_in(3 - k)

    relay_from = 4 - 3 * k
    for part in range(2):
        arrived(relay_from, part)
        go(move(relay_from, 6, part, 10 + part, far))
        arrived(5 * k, part)
        go(move(k, k, part, 12 + part, partner))
        go(move(4 + k, 4 + k, part, 14 + part, partner))

    @pl.when(has_below)
    def _():
        to_above.wait_recv()

    @pl.when(has_above)
    def _():
        to_below.wait_recv()

    def second_copy(src, dst, number, peer):
        return remote(src, dst, send2.at[number], recv2.at[number], peer)

    xe[0:NB, :] = jnp.dot(tbuf[7 - k], win[8 - k, 0:NB, :], preferred_element_type=F32).astype(BF)
    xe[NB:ROWS, :] = win[8 - k, NB:ROWS, :]
    pair_e = go(second_copy(xe, pe, 0, partner))
    acc_e[...] = jnp.dot(tbuf[6 + k], win[7 + k, 0:NB, :], preferred_element_type=F32)
    mine_row = row_of(own)
    their_row = row_of(3 - k)
    edge_row = row_of(7 + k)
    pair_e.wait_recv()
    edge_row2 = pe[NB:ROWS, :].astype(F32)[0:1, :]

    @pl.loop(0, 2 * SIDE)
    def _(block):
        rows = pl.ds(pl.multiple_of(block * BAND, BAND), BAND)
        e1 = acc_e[rows, :]
        e2 = pe[rows, :].astype(F32)
        for coarse in range(2):
            w1 = mine_row if coarse else 1.0 - mine_row
            w2 = their_row if coarse else 1.0 - their_row
            to_x = 2 * coarse + block // SIDE
            to_y = lax.rem(block, SIDE)
            u = to_x * fx + to_y * fy
            v = to_x * fy + to_y * fx
            dense_e[u, v, :, 0:NB] = (e1 * (w1 * (1.0 - edge_row)) + e2 * (w2 * (1.0 - edge_row2))).astype(BF)
            dense_e[u, v, :, NB:2 * NB] = (e1 * (w1 * edge_row) + e2 * (w2 * edge_row2)).astype(BF)

    lo, hi = pl.ds(0, 2), pl.ds(2, 2)

    class Ring:
        def __init__(self, buf, far_buf, near_buf, total, me, line, number):
            self.buf, self.far, self.near, self.total, self.me = buf, far_buf, near_buf, total, me
            self.plus, self.minus, self.number = line[0], line[2], number
            self.up = lax.rem(me + 1, SIDE)
            self.opposite = lax.rem(me + 2, SIDE)
            self.down = lax.rem(me + 3, SIDE)

        def begin(self):
            n, buf = self.number, self.buf
            self.first = [
                go(second_copy(buf.at[self.opposite, lo], self.far.at[0], n, self.plus)),
                go(second_copy(buf.at[self.opposite, hi], self.far.at[1], n + 1, self.minus)),
            ]
            self.rest = [
                go(second_copy(buf.at[self.up, hi], self.near.at[0, hi], n + 2, self.plus)),
                go(second_copy(buf.at[self.down, lo], self.near.at[1, lo], n + 3, self.minus)),
            ]

        def relay(self):
            n, buf = self.number, self.buf
            self.first[0].wait_recv()
            for v in range(2):
                buf[self.up, v] = (buf[self.up, v].astype(F32) + self.far[0, v].astype(F32)).astype(BF)
            self.rest.append(go(second_copy(buf.at[self.up, lo], self.near.at[0, lo], n + 4, self.plus)))
            self.first[1].wait_recv()
            for v in range(2):
                buf[self.down, 2 + v] = (
                    buf[self.down, 2 + v].astype(F32) + self.far[1, v].astype(F32)
                ).astype(BF)
            self.rest.append(go(second_copy(buf.at[self.down, hi], self.near.at[1, hi], n + 5, self.minus)))

        def end(self):
            for copy in self.rest:
                copy.wait_recv()

            @pl.loop(0, SIDE)
            def _(v):
                self.total[v] = (
                    self.buf[self.me, v].astype(F32) + self.near[0, v].astype(F32) + self.near[1, v].astype(F32)
                ).astype(BF)

    ring_e = Ring(dense_e, far_e, near_e, sum_e, first_at, first_line, 2)
    ring_m = Ring(dense_m, far_m, near_m, sum_m, first_at, first_line, 8)
    ring_e.begin()

    take_in(k)
    take_in(4 + k)
    for slot in (1 - k, 5 - k, 6):
        for part in range(2):
            arrived(slot, part)
        take_in(slot)
    xm[...] = acc[1 - k].astype(BF)
    pair_m = go(second_copy(xm, pm, 1, partner))
    ring_e.relay()
    pair_m.wait_recv()

    @pl.loop(0, 2 * SIDE)
    def _(block):
        rows = pl.ds(pl.multiple_of(block * BAND, BAND), BAND)
        m1 = acc[k, rows, :]
        m2 = pm[rows, :].astype(F32)
        for coarse in range(2):
            w1 = mine_row if coarse else 1.0 - mine_row
            w2 = their_row if coarse else 1.0 - their_row
            to_x = 2 * coarse + block // SIDE
            to_y = lax.rem(block, SIDE)
            dense_m[to_x * fx + to_y * fy, to_x * fy + to_y * fx] = (m1 * w1 + m2 * w2).astype(BF)

    ring_m.begin()

    def spread(total, last, me, line, number):
        return [
            go(second_copy(total.at[lax.rem(me + step, SIDE)], last.at[step - 1], number + step, line[step - 1]))
            for step in (2, 1, 3)
        ]

    ring_e.end()
    lasts = spread(sum_e, last_e, second_at, second_line, 13)
    ring_m.relay()
    ring_m.end()
    lasts = lasts + spread(sum_m, last_m, second_at, second_line, 16)
    for copy in lasts:
        copy.wait_recv()

    def closed(total, last, me, width):
        value = total[me].astype(F32)
        for number in range(3):
            value = value + last[number].astype(F32)
        return value.reshape(2, BAND // 2, width)

    fin[:, :, 0:2 * NB] = closed(sum_e, last_e, second_at, 2 * NB)
    fin[:, :, 2 * NB:HALF] = closed(sum_m, last_m, second_at, NB)
    swap = go(second_copy(fin.at[1 - k], got_fin, 20, partner))

    def place_half(side, ref):
        edge_at = side * (HALF + NB)
        mid_at = 2 * NB + side * NB
        out[:, pl.ds(pl.multiple_of(edge_at, 128), 2 * NB)] = ref[:, 0:2 * NB]
        out[:, pl.ds(pl.multiple_of(mid_at, 128), NB)] = ref[:, 2 * NB:HALF]

    place_half(k, fin.at[k])
    swap.wait_recv()
    place_half(1 - k, got_fin)

    @pl.when(has_above)
    def _():
        to_above.wait_send()

    @pl.when(has_below)
    def _():
        to_below.wait_send()

    for copy in sent:
        copy.wait_send()


def ring_buffers(width):
    return [
        pltpu.VMEM((SIDE, SIDE, BAND, width), BF),
        pltpu.VMEM((2, 2, BAND, width), BF),
        pltpu.VMEM((2, SIDE, BAND, width), BF),
        pltpu.VMEM((SIDE, BAND, width), BF),
        pltpu.VMEM((3, BAND, width), BF),
    ]


def on_device(stiff_rows, stiff_iface, columns, live_count, aggregate, prolong):
    smem = pl.BlockSpec(memory_space=pltpu.SMEM)
    anywhere = pl.BlockSpec(memory_space=pl.ANY)
    return pl.pallas_call(
        kernel,
        out_shape=jax.ShapeDtypeStruct((BAND // 2, 2 * HALF), F32),
        in_specs=[smem, smem, smem, anywhere, anywhere, anywhere],
        out_specs=pl.BlockSpec(memory_space=pltpu.VMEM),
        scratch_shapes=[
            pltpu.VMEM((9, ROWS, NB), BF),
            pltpu.VMEM((SLOTS + 2, NB, NB), BF),
            pltpu.VMEM((NB, NB), BF),
            pltpu.VMEM((SLOTS + 2, NB, NB), BF),
            pltpu.VMEM((2, NB, NB), F32),
            pltpu.VMEM((NB, NB), F32),
            pltpu.VMEM((ROWS, NB), BF),
            pltpu.VMEM((ROWS, NB), BF),
            pltpu.VMEM((NB, NB), BF),
            pltpu.VMEM((NB, NB), BF),
            *ring_buffers(2 * NB),
            *ring_buffers(NB),
            pltpu.VMEM((2, BAND // 2, HALF), F32),
            pltpu.VMEM((BAND // 2, HALF), F32),
            pltpu.SemaphoreType.DMA((3,)),
            pltpu.SemaphoreType.DMA((16,)),
            pltpu.SemaphoreType.DMA((9, 2)),
            pltpu.SemaphoreType.DMA((21,)),
            pltpu.SemaphoreType.DMA((21,)),
        ],
        compiler_params=pltpu.CompilerParams(
            collective_id=0, has_side_effects=True, vmem_limit_bytes=60 * 1024 * 1024
        ),
        name="coarse",
    )(columns, live_count, aggregate, stiff_rows, stiff_iface, prolong)


def solution(mesh):
    in_specs = (
        P(("grp", "dev"), None, None, None),
        P(("grp", "dev"), None, None, None),
        P(("grp", "dev"), None),
        P(("grp", "dev")),
        P(("grp", "dev")),
        P(("grp", "dev"), None, None),
    )
    out_specs = P(("grp", "dev"), None)
    return jax.shard_map(
        on_device, mesh=mesh, in_specs=in_specs, out_specs=out_specs, check_vma=False
    )
```

```python
import jax
import jax.numpy as jnp
from jax import lax
from jax.experimental import pallas as pl
from jax.experimental.pallas import tpu as pltpu
from jax.sharding import PartitionSpec as P

NB = 384
SLOTS = 6
TAIL = 16
ROWS = NB + TAIL
CUT = 192
SIDE = 4
BAND = 48
HALF = 3 * NB
MESH = pl.DeviceIdType.MESH
BF = jnp.bfloat16
F32 = jnp.float32


def kernel(
    cols, live, agg, stiff_rows, stiff_iface, prolong, out,
    win, bbuf, pt, tbuf, acc, acc_f, tf_out, tf_in, acc_e, xe, pe, xm, pm,
    dense_e, far_e, near_e, sum_e, last_e, dense_m, far_m, near_m, sum_m, last_m, fin, got_fin,
    load_sem, send_sem, recv_sem, send2, recv2,
):
    g = lax.axis_index("grp")
    d = lax.axis_index("dev")
    groups = lax.axis_size("grp")
    devs = lax.axis_size("dev")
    k = lax.rem(d, 2)
    c = d // 2
    chips = devs // 2
    x = c // SIDE
    y = lax.rem(c, SIDE)
    own = 2 + k

    fx, fy = 1 - k, k

    def at(cx, cy):
        return (g, (lax.rem(cx, SIDE) * SIDE + lax.rem(cy, SIDE)) * 2 + k)

    partner = (g, c * 2 + 1 - k)
    nxt = (g, lax.rem(c + 1, chips) * 2 + k)
    prv = (g, lax.rem(c + chips - 1, chips) * 2 + k)
    far = (g, lax.rem(c + chips + 2 * k - 1, chips) * 2 + 1 - k)
    above = (jnp.minimum(g + 1, groups - 1), d)
    below = (jnp.maximum(g - 1, 0), d)
    has_above = g < groups - 1
    has_below = g > 0
    first_at = x * fx + y * fy
    second_at = x * fy + y * fx
    first_line = [at(x + s * fx, y + s * fy) for s in (1, 2, 3)]
    second_line = [at(x + s * fy, y + s * fx) for s in (1, 2, 3)]

    load_p = pltpu.make_async_copy(prolong.at[0], win.at[own, pl.ds(0, NB)], load_sem.at[0])
    load_b = pltpu.make_async_copy(stiff_rows.at[0], bbuf.at[pl.ds(0, SLOTS)], load_sem.at[1])
    load_i = pltpu.make_async_copy(stiff_iface.at[0], bbuf.at[pl.ds(SLOTS, 2)], load_sem.at[2])
    load_p.start()

    barrier = pltpu.get_barrier_semaphore()
    peers = [partner, nxt, prv, far] + first_line + second_line

    @pl.when(has_above)
    def _():
        pl.semaphore_signal(barrier, inc=1, device_id=above, device_id_type=MESH)

    @pl.when(has_below)
    def _():
        pl.semaphore_signal(barrier, inc=1, device_id=below, device_id_type=MESH)

    for peer in peers:
        pl.semaphore_signal(barrier, inc=1, device_id=peer, device_id_type=MESH)
    win[own, NB:ROWS, :] = jnp.full((TAIL, NB), agg[0].astype(F32), F32).astype(BF)

    @pl.when(jnp.logical_not(has_below))
    def _():
        win[7] = jnp.zeros((ROWS, NB), BF)

    @pl.when(jnp.logical_not(has_above))
    def _():
        win[8] = jnp.zeros((ROWS, NB), BF)

    load_p.wait()
    load_b.start()
    load_i.start()
    pl.semaphore_wait(barrier, len(peers) + has_above.astype(jnp.int32) + has_below.astype(jnp.int32))

    parts = (pl.ds(0, CUT), pl.ds(CUT, ROWS - CUT))

    def remote(src, dst, sems, rems, peer):
        return pltpu.make_async_remote_copy(
            src_ref=src, dst_ref=dst, send_sem=sems, recv_sem=rems, device_id=peer, device_id_type=MESH
        )

    sent = []

    def go(copy):
        copy.start()
        sent.append(copy)
        return copy

    def move(src_slot, dst_slot, part, number, peer):
        return remote(
            win.at[src_slot, parts[part]], win.at[dst_slot, parts[part]],
            send_sem.at[number], recv_sem.at[dst_slot, part], peer,
        )

    def arrived(slot, part):
        move(slot, slot, part, 0, partner).wait_recv()

    to_above = remote(win.at[own], win.at[7], send_sem.at[4], recv_sem.at[7, 0], above)
    to_below = remote(win.at[own], win.at[8], send_sem.at[5], recv_sem.at[8, 0], below)
    for part in range(2):
        go(move(own, k, part, part, nxt))
        go(move(own, 4 + k, part, 2 + part, prv))

    @pl.when(has_above)
    def _():
        to_above.start()

    @pl.when(has_below)
    def _():
        to_below.start()

    for part in range(2):
        go(move(own, own, part, 8 + part, partner))

    pt[...] = win[own, 0:NB, :].astype(F32).T.astype(BF)
    load_b.wait()
    load_i.wait()

    @pl.loop(0, SLOTS + 2)
    def _(index):
        tbuf[index] = jnp.dot(pt[...], bbuf[index], preferred_element_type=F32).astype(BF)

    base = 2 * c
    live_now = live[0]
    slot_of = []
    for index in range(SLOTS):
        rel = lax.rem(cols[0, index] - base + 2 + 2 * devs, devs)
        slot_of.append(jnp.minimum(rel, 6))

    def row_of(slot):
        return win[slot, NB:ROWS, :].astype(F32)[0:1, :]

    def found(slot):
        index = jnp.int32(0)
        weight = jnp.int32(0)
        for number in range(SLOTS):
            hit = (slot_of[number] == slot).astype(jnp.int32)
            index = index + hit * number
            weight = weight + hit * (number < live_now).astype(jnp.int32)
        return jnp.minimum(index, SLOTS - 1), weight.astype(F32)

    index, scale = found(6)
    tf_out[0:NB, :] = (tbuf[index].astype(F32) * scale).astype(BF)
    tf_out[NB:ROWS, :] = win[own, NB:ROWS, :]
    far_product = go(remote(tf_out, tf_in, send_sem.at[10], recv_sem.at[6, 0], far))

    def take_in(slot, fresh=False):
        index, scale = found(slot)
        high = row_of(slot) * scale
        low = scale - high
        value = jnp.dot(tbuf[index], win[slot, 0:NB, :], preferred_element_type=F32)
        if fresh:
            acc[0] = value * low
            acc[1] = value * high
        else:
            acc[0] += value * low
            acc[1] += value * high

    take_in(own, True)
    for part in range(2):
        arrived(3 - k, part)
    take_in(3 - k)

    relay_from = 4 - 3 * k
    for part in range(2):
        arrived(relay_from, part)
        arrived(5 * k, part)
        go(move(k, k, part, 12 + part, partner))
        go(move(4 + k, 4 + k, part, 14 + part, partner))

    @pl.when(has_below)
    def _():
        to_above.wait_recv()

    @pl.when(has_above)
    def _():
        to_below.wait_recv()

    def second_copy(src, dst, number, peer):
        return remote(src, dst, send2.at[number], recv2.at[number], peer)

    xe[0:NB, :] = jnp.dot(tbuf[7 - k], win[8 - k, 0:NB, :], preferred_element_type=F32).astype(BF)
    xe[NB:ROWS, :] = win[8 - k, NB:ROWS, :]
    pair_e = go(second_copy(xe, pe, 0, partner))
    acc_e[...] = jnp.dot(tbuf[6 + k], win[7 + k, 0:NB, :], preferred_element_type=F32)
    mine_row = row_of(own)
    their_row = row_of(3 - k)
    edge_row = row_of(7 + k)
    pair_e.wait_recv()
    edge_row2 = pe[NB:ROWS, :].astype(F32)[0:1, :]

    @pl.loop(0, 2 * SIDE)
    def _(block):
        rows = pl.ds(pl.multiple_of(block * BAND, BAND), BAND)
        e1 = acc_e[rows, :]
        e2 = pe[rows, :].astype(F32)
        for coarse in range(2):
            w1 = mine_row if coarse else 1.0 - mine_row
            w2 = their_row if coarse else 1.0 - their_row
            to_x = 2 * coarse + block // SIDE
            to_y = lax.rem(block, SIDE)
            u = to_x * fx + to_y * fy
            v = to_x * fy + to_y * fx
            dense_e[u, v, :, 0:NB] = (e1 * (w1 * (1.0 - edge_row)) + e2 * (w2 * (1.0 - edge_row2))).astype(BF)
            dense_e[u, v, :, NB:2 * NB] = (e1 * (w1 * edge_row) + e2 * (w2 * edge_row2)).astype(BF)

    lo, hi = pl.ds(0, 2), pl.ds(2, 2)

    class Ring:
        def __init__(self, buf, far_buf, near_buf, total, me, line, number):
            self.buf, self.far, self.near, self.total, self.me = buf, far_buf, near_buf, total, me
            self.plus, self.minus, self.number = line[0], line[2], number
            self.up = lax.rem(me + 1, SIDE)
            self.opposite = lax.rem(me + 2, SIDE)
            self.down = lax.rem(me + 3, SIDE)

        def begin(self):
            n, buf = self.number, self.buf
            self.first = [
                go(second_copy(buf.at[self.opposite, lo], self.far.at[0], n, self.plus)),
                go(second_copy(buf.at[self.opposite, hi], self.far.at[1], n + 1, self.minus)),
            ]
            self.rest = [
                go(second_copy(buf.at[self.up, hi], self.near.at[0, hi], n + 2, self.plus)),
                go(second_copy(buf.at[self.down, lo], self.near.at[1, lo], n + 3, self.minus)),
            ]

        def relay(self):
            n, buf = self.number, self.buf
            self.first[0].wait_recv()
            for v in range(2):
                buf[self.up, v] = (buf[self.up, v].astype(F32) + self.far[0, v].astype(F32)).astype(BF)
            self.rest.append(go(second_copy(buf.at[self.up, lo], self.near.at[0, lo], n + 4, self.plus)))
            self.first[1].wait_recv()
            for v in range(2):
                buf[self.down, 2 + v] = (
                    buf[self.down, 2 + v].astype(F32) + self.far[1, v].astype(F32)
                ).astype(BF)
            self.rest.append(go(second_copy(buf.at[self.down, hi], self.near.at[1, hi], n + 5, self.minus)))

        def end(self):
            for copy in self.rest:
                copy.wait_recv()

            @pl.loop(0, SIDE)
            def _(v):
                self.total[v] = (
                    self.buf[self.me, v].astype(F32) + self.near[0, v].astype(F32) + self.near[1, v].astype(F32)
                ).astype(BF)

    ring_e = Ring(dense_e, far_e, near_e, sum_e, first_at, first_line, 2)
    ring_m = Ring(dense_m, far_m, near_m, sum_m, first_at, first_line, 8)
    ring_e.begin()

    take_in(k)
    take_in(4 + k)
    for slot in (1 - k, 5 - k):
        for part in range(2):
            arrived(slot, part)
        take_in(slot)
    far_product.wait_recv()
    value = jnp.dot(tf_in[0:NB, :], win[relay_from, 0:NB, :], preferred_element_type=F32)
    high = row_of(relay_from)
    acc_f[0] = value * (1.0 - high)
    acc_f[1] = value * high
    xm[0, 0:NB, :] = acc[1 - k].astype(BF)
    xm[0, NB:ROWS, :] = jnp.zeros((TAIL, NB), BF)
    xm[1, 0:NB, :] = acc_f[1 - k].astype(BF)
    xm[1, NB:ROWS, :] = tf_in[NB:ROWS, :]
    pair_m = go(second_copy(xm, pm, 1, partner))
    ring_e.relay()
    pair_m.wait_recv()
    far_row = tf_in[NB:ROWS, :].astype(F32)[0:1, :]
    far_row2 = pm[1, NB:ROWS, :].astype(F32)[0:1, :]

    @pl.loop(0, 2 * SIDE)
    def _(block):
        rows = pl.ds(pl.multiple_of(block * BAND, BAND), BAND)
        m1 = acc[k, rows, :]
        m2 = pm[0, rows, :].astype(F32)
        m3 = acc_f[k, rows, :]
        m4 = pm[1, rows, :].astype(F32)
        for coarse in range(2):
            w1 = mine_row if coarse else 1.0 - mine_row
            w2 = their_row if coarse else 1.0 - their_row
            w3 = far_row if coarse else 1.0 - far_row
            w4 = far_row2 if coarse else 1.0 - far_row2
            to_x = 2 * coarse + block // SIDE
            to_y = lax.rem(block, SIDE)
            dense_m[to_x * fx + to_y * fy, to_x * fy + to_y * fx] = (
                m1 * w1 + m2 * w2 + m3 * w3 + m4 * w4
            ).astype(BF)

    ring_m.begin()

    def spread(total, last, me, line, number):
        return [
            go(second_copy(total.at[lax.rem(me + step, SIDE)], last.at[step - 1], number + step, line[step - 1]))
            for step in (2, 1, 3)
        ]

    ring_e.end()
    lasts = spread(sum_e, last_e, second_at, second_line, 13)
    ring_m.relay()
    ring_m.end()
    lasts = lasts + spread(sum_m, last_m, second_at, second_line, 16)
    for copy in lasts:
        copy.wait_recv()

    def closed(total, last, me, width):
        value = total[me].astype(F32)
        for number in range(3):
            value = value + last[number].astype(F32)
        return value.reshape(2, BAND // 2, width)

    fin[:, :, 0:2 * NB] = closed(sum_e, last_e, second_at, 2 * NB)
    fin[:, :, 2 * NB:HALF] = closed(sum_m, last_m, second_at, NB)
    swap = go(second_copy(fin.at[1 - k], got_fin, 20, partner))

    def place_half(side, ref):
        edge_at = side * (HALF + NB)
        mid_at = 2 * NB + side * NB
        out[:, pl.ds(pl.multiple_of(edge_at, 128), 2 * NB)] = ref[:, 0:2 * NB]
        out[:, pl.ds(pl.multiple_of(mid_at, 128), NB)] = ref[:, 2 * NB:HALF]

    place_half(k, fin.at[k])
    swap.wait_recv()
    place_half(1 - k, got_fin)

    @pl.when(has_above)
    def _():
        to_above.wait_send()

    @pl.when(has_below)
    def _():
        to_below.wait_send()

    for copy in sent:
        copy.wait_send()


def ring_buffers(width):
    return [
        pltpu.VMEM((SIDE, SIDE, BAND, width), BF),
        pltpu.VMEM((2, 2, BAND, width), BF),
        pltpu.VMEM((2, SIDE, BAND, width), BF),
        pltpu.VMEM((SIDE, BAND, width), BF),
        pltpu.VMEM((3, BAND, width), BF),
    ]


def on_device(stiff_rows, stiff_iface, columns, live_count, aggregate, prolong):
    smem = pl.BlockSpec(memory_space=pltpu.SMEM)
    anywhere = pl.BlockSpec(memory_space=pl.ANY)
    return pl.pallas_call(
        kernel,
        out_shape=jax.ShapeDtypeStruct((BAND // 2, 2 * HALF), F32),
        in_specs=[smem, smem, smem, anywhere, anywhere, anywhere],
        out_specs=pl.BlockSpec(memory_space=pltpu.VMEM),
        scratch_shapes=[
            pltpu.VMEM((9, ROWS, NB), BF),
            pltpu.VMEM((SLOTS + 2, NB, NB), BF),
            pltpu.VMEM((NB, NB), BF),
            pltpu.VMEM((SLOTS + 2, NB, NB), BF),
            pltpu.VMEM((2, NB, NB), F32),
            pltpu.VMEM((2, NB, NB), F32),
            pltpu.VMEM((ROWS, NB), BF),
            pltpu.VMEM((ROWS, NB), BF),
            pltpu.VMEM((NB, NB), F32),
            pltpu.VMEM((ROWS, NB), BF),
            pltpu.VMEM((ROWS, NB), BF),
            pltpu.VMEM((2, ROWS, NB), BF),
            pltpu.VMEM((2, ROWS, NB), BF),
            *ring_buffers(2 * NB),
            *ring_buffers(NB),
            pltpu.VMEM((2, BAND // 2, HALF), F32),
            pltpu.VMEM((BAND // 2, HALF), F32),
            pltpu.SemaphoreType.DMA((3,)),
            pltpu.SemaphoreType.DMA((16,)),
            pltpu.SemaphoreType.DMA((9, 2)),
            pltpu.SemaphoreType.DMA((21,)),
            pltpu.SemaphoreType.DMA((21,)),
        ],
        compiler_params=pltpu.CompilerParams(
            collective_id=0, has_side_effects=True, vmem_limit_bytes=60 * 1024 * 1024
        ),
        name="coarse",
    )(columns, live_count, aggregate, stiff_rows, stiff_iface, prolong)


def solution(mesh):
    in_specs = (
        P(("grp", "dev"), None, None, None),
        P(("grp", "dev"), None, None, None),
        P(("grp", "dev"), None),
        P(("grp", "dev")),
        P(("grp", "dev")),
        P(("grp", "dev"), None, None),
    )
    out_specs = P(("grp", "dev"), None)
    return jax.shard_map(
        on_device, mesh=mesh, in_specs=in_specs, out_specs=out_specs, check_vma=False
    )
```
